128 devices in a mesh: ep: 32 (over z, y, core), dp: 4 (over x).
Axes of the slice: x: 4, y: 4, z: 4, core: 2. Of those that a mesh axis runs over, the one named last changes fastest.
Arguments:
- tokens: bfloat16 [2048, 7168], P(('ep', 'dp')), may hold values from -6 to 6
- routes: int32 [2048, 8], P(('ep', 'dp')), may hold values from 0 to 31, all different within a row; in each aligned block of 16 rows (0 to 15, 16 to 31, ...) at most 8 rows name the same one
- route_logits: float32 [2048, 8], P(('ep', 'dp')), may hold values from -6 to 6
- gate_weight: bfloat16 [32, 7168, 2048], P('ep', None, 'dp'), may hold values from -0.0625 to 0.0625
- up_weight: bfloat16 [32, 7168, 2048], P('ep', None, 'dp'), may hold values from -0.0625 to 0.0625
- down_weight: bfloat16 [32, 2048, 7168], P('ep', 'dp'), may hold values from -0.125 to 0.125
Outputs:
- moe_output: bfloat16 [2048, 7168], P(('ep', 'dp'))
- expert_load: float32 [32], P('ep')
The draws below stay inside these ranges and needn't reach their ends.
Inputs may be any that keep to these rules, and one draw needn't show every extreme that they name: `routes`: each row names 8 different experts. Within the rows of one device (aligned blocks of 16 rows) no expert is named more than 8 times, and in every draw some expert is named exactly 8 times there; every expert is named somewhere.
All inputs are finite; a program needn't handle non-finite values.
Results may differ from the reference program's by a relative error of at most 0.012.
Values may be sent and summed in bfloat16 or wider, within the bound.
No kernel may reach another device: no remote copies, remote signals or barrier semaphores. Data moves between devices by JAX's collectives and lax.ppermute only.
A program may use at most 128 MiB of HBM per device.

```python
import math
import jax
import jax.numpy as jnp
import numpy as np
from jax import lax

D = 7168
FF = 2048
TOK_DEV = 16
EXPERTS = 32
TOP = 8
CAP = 8
TOKENS = 2048
N_EP = 32
N_DP = 4


def levels(key, extent, split, smallest, high):
    level, own = 1.0, jax.random.fold_in(key, 6)
    for dim, shards_of in split:
        heights = jnp.exp(jax.random.uniform(jax.random.fold_in(own, dim), (shards_of,), jnp.float32, smallest / len(split), high / len(split)))
        level = level * jnp.repeat(heights, extent[dim] // shards_of).reshape([-1 if axis == dim else 1 for axis in range(len(extent))])
    return level


def assign_block(rng, own, number, rows, amount, top, bound, slope):
    sequence = jax.random.permutation(rng, amount)
    packed, common = load_shares(amount, rows * top, bound, slope, True), load_shares(amount, rows * top, bound, slope, False)
    places = jnp.arange(amount)

    def named(tallies, turn):
        used = int((tallies > 0).sum())
        fixed = max(1, used // 4)
        passed = fixed + (places - fixed + turn * (used - fixed)) % max(1, amount - fixed)
        return jnp.zeros((amount,), jnp.int32).at[sequence[jnp.where(places < fixed, places, passed)]].set(jnp.asarray(tallies, jnp.int32))

    tallies = jnp.where(number % 4 == 0, named(packed, number // 4), named(common, number - number // 4 - 1))
    mixed = jax.random.permutation(jax.random.fold_in(own, 3), amount)
    source_of, receiver = mixed[0:amount // 2 * 2:2], mixed[1:amount // 2 * 2:2]
    margin = jnp.minimum(tallies[source_of] - 1, bound - tallies[receiver]) // 2
    margin = jnp.where((source_of == sequence[0]) | (receiver == sequence[0]) | (tallies[receiver] == 0), 0, jnp.maximum(margin, 0))
    passed = jax.random.randint(jax.random.fold_in(own, 4), (amount // 2,), 0, 1 << 20) % (margin + 1)
    tallies = tallies.at[source_of].add(-passed).at[receiver].add(passed)
    items = jnp.searchsorted(jnp.cumsum(tallies), jnp.arange(rows * top), side="right").astype(jnp.int32)
    table = items.reshape(top, rows).T
    table = table[jax.random.permutation(jax.random.fold_in(own, 1), rows)]
    turn = jax.random.randint(jax.random.fold_in(own, 2), (rows, 1), 0, top)
    return jnp.take_along_axis(table, (jnp.arange(top)[None, :] + turn) % top, axis=1)


def load_shares(amount, total, most, lean, full):
    portions = [(1 << 20) // math.isqrt(standing ** lean) + 1 for standing in range(1, amount + 1)]
    largest = most if full else min(most, max(-(-total // amount), total * portions[0] // sum(portions)))
    least = 1 if total - largest >= amount - 1 else 0
    given, rest = [largest] + [least] * (amount - 1), total - largest - least * (amount - 1)
    while rest > 0:
        movable = [i for i in range(1, amount) if given[i] < largest] or [i for i in range(1, amount) if given[i] < most]
        whole, left = sum([portions[i] for i in movable]), rest
        for i in movable:
            extra = min(most - given[i], max(1, left * portions[i] // whole), rest)
            given[i] = given[i] + extra
            rest = rest - extra
    return np.array(given)


def scatter_about(rng, shape, spread, limit, split=(), held_as=jnp.bfloat16):
    loudness = levels(rng, shape, split, -0.22, 0.18) if split else 1.0
    drawn = jax.random.normal(rng, shape, jnp.float32) * spread * loudness
    return jnp.minimum(jnp.maximum(drawn, -limit), limit).astype(held_as)


def setup_inputs(seed: int = 0) -> dict:
    splits = jax.random.split(jax.random.key(seed), 7)
    tokens = scatter_about(splits[0], (TOKENS, D), 1.0, 6.0, ((0, 128),))
    routes_keys = jax.random.split(jax.random.fold_in(splits[1], 1), TOKENS // TOK_DEV)
    routes_turns = jax.random.permutation(jax.random.fold_in(splits[1], 3), TOKENS // TOK_DEV)
    routes = jax.vmap(lambda own, number: assign_block(jax.random.fold_in(splits[1], 2), own, number, TOK_DEV, EXPERTS, TOP, CAP, 2))(routes_keys, routes_turns).reshape((TOKENS, TOP))
    route_logits = scatter_about(splits[2], (TOKENS, TOP), 1.5, 6.0, ((0, 128),), jnp.float32)
    gate_weight = scatter_about(splits[3], (EXPERTS, D, FF), D ** -0.5, 0.0625, ((0, 32), (2, 4)))
    up_weight = scatter_about(splits[4], (EXPERTS, D, FF), D ** -0.5, 0.0625, ((0, 32), (2, 4)))
    down_weight = scatter_about(splits[5], (EXPERTS, FF, D), FF ** -0.5, 0.125, ((0, 32), (1, 4)))
    return dict(tokens=tokens, routes=routes, route_logits=route_logits, gate_weight=gate_weight, up_weight=up_weight, down_weight=down_weight)


ROUTE_SCALE = 2.5


def reference(tokens, routes, route_logits, gate_weight, up_weight, down_weight):
    device_count = N_EP * N_DP
    per_block = TOK_DEV * TOP
    quarter = FF // N_DP
    flat_routes = routes.reshape(device_count, per_block)
    labels = jnp.arange(EXPERTS, dtype=jnp.int32)
    onehot = (flat_routes[:, :, None] == labels[None, None, :]).astype(jnp.int32)
    slot_ids = jnp.sum((jnp.cumsum(onehot, axis=1) - onehot) * onehot, axis=2)
    expert_count = jnp.sum(onehot, axis=(0, 1)).astype(jnp.float32)
    affinity = jax.nn.sigmoid(route_logits)
    weights = ROUTE_SCALE * affinity / jnp.sum(affinity, axis=1, keepdims=True)
    device_ids = jnp.arange(device_count, dtype=jnp.int32)[:, None]
    token_ids = device_ids * TOK_DEV + jnp.arange(per_block, dtype=jnp.int32)[None, :] // TOP
    position = ((flat_routes * device_count + device_ids) * CAP + slot_ids).reshape(-1).astype(jnp.int32)
    token_table = jnp.zeros((EXPERTS * device_count * CAP,), jnp.int32).at[position].set(token_ids.reshape(-1).astype(jnp.int32))
    weight_table = jnp.zeros((EXPERTS * device_count * CAP,), jnp.float32).at[position].set(weights.reshape(-1))
    token_table = token_table.reshape(EXPERTS, device_count * CAP)
    weight_table = weight_table.reshape(EXPERTS, device_count * CAP)

    def expert_step(running, inputs):
        row_index, slot_weight, gate_w, up_w, down_w = inputs
        row_block = tokens[row_index]
        gate_act = jnp.dot(row_block, gate_w, preferred_element_type=jnp.float32)
        up_act = jnp.dot(row_block, up_w, preferred_element_type=jnp.float32)
        hidden = (jax.nn.silu(gate_act) * up_act).astype(jnp.bfloat16)
        pieces = []
        for index_q in range(N_DP):
            lower = index_q * quarter
            piece = jnp.dot(hidden[:, lower:lower + quarter], down_w[lower:lower + quarter], preferred_element_type=jnp.float32)
            pieces.append(piece.astype(jnp.bfloat16))
        pieces = lax.optimization_barrier(pieces)
        expert_out = pieces[0].astype(jnp.float32)
        for piece in pieces[1:]:
            expert_out = expert_out + piece.astype(jnp.float32)
        return running.at[row_index].add(expert_out * slot_weight[:, None]), None

    running, _ = lax.scan(expert_step, jnp.zeros((TOKENS, D), jnp.float32), (token_table, weight_table, gate_weight, up_weight, down_weight))
    moe_output = running.astype(jnp.bfloat16)
    mean_count = float(TOK_DEV * N_DP * TOP)
    expert_load = expert_count / mean_count
    return moe_output, expert_load
```

```python
import jax
import jax.numpy as jnp
from jax import lax
from jax.experimental import pallas as pl
from jax.experimental.pallas import tpu as pltpu
from jax.sharding import Mesh
from jax.sharding import PartitionSpec as P

EP = ("z", "y", "c")
EP_DP = ("z", "y", "c", "x")
ROUTE_SCALE = 2.5
EXTRA = 128
SIDE = 4
GATHER = (("x", "y", "z"), ("y", "z", "x"), ("z", "x", "y"))
REDUCE = (("z", "y", "x"), ("x", "z", "y"), ("y", "x", "z"))
DIM = {"z": 0, "y": 1, "x": 2}


def ring(v, axis, sign):
    pairs = []
    for i in range(SIDE):
        for core in range(2):
            step = sign if core == 0 else -sign
            j = (i + step) % SIDE
            if axis == "x":
                pairs.append((core * SIDE + i, core * SIDE + j))
            else:
                pairs.append((i * 2 + core, j * 2 + core))
    return lax.ppermute(v, ("c", "x") if axis == "x" else (axis, "c"), pairs)


def swap(v):
    return lax.ppermute(v, "c", [(0, 1), (1, 0)])


def route_columns(routes, route_logits, experts):
    affinity = jax.nn.sigmoid(route_logits)
    weights = ROUTE_SCALE * affinity / jnp.sum(affinity, axis=1, keepdims=True)
    hit = routes[:, :, None] == jnp.arange(experts, dtype=jnp.int32)[None, None, :]
    mask = jnp.sum(hit.astype(jnp.float32), axis=1)
    dense = jnp.sum(jnp.where(hit, weights[:, :, None], 0.0), axis=1)
    high = lax.reduce_precision(dense, 8, 7)
    rest = dense - high
    mid = lax.reduce_precision(rest, 8, 7)
    low = rest - mid
    return jnp.concatenate([mask, high, mid, low], axis=1).astype(jnp.bfloat16)


def back(i):
    return (SIDE - i) % SIDE


def combine_kernel(*refs):
    gates, ups = refs[:24], refs[24:48]
    route = refs[48:56]
    mine_ref, send_ref, count_ref = refs[56:59]
    gate_buf, up_buf, route_buf, sems = refs[59:]

    def copies(tile, slot):
        lst, i = divmod(tile, SIDE)
        out = []
        for which, (parts, buf) in enumerate(((gates, gate_buf), (ups, up_buf))):
            sem = sems.at[slot, which]
            first, second, third = (parts[t * 8 + lst * 4 : t * 8 + lst * 4 + 4] for t in range(3))
            out.append(pltpu.make_async_copy(first[i], buf.at[slot, 0], sem.at[0]))
            for r in range(SIDE):
                out.append(
                    pltpu.make_async_copy(second[r].at[i], buf.at[slot, 1, :, r], sem.at[1 + r])
                )
                out.append(
                    pltpu.make_async_copy(third[r].at[:, i], buf.at[slot, 2, r], sem.at[5 + r])
                )
        for r in range(SIDE):
            out.append(
                pltpu.make_async_copy(
                    route[lst * 4 + r].at[:, i], route_buf.at[slot, r], sems.at[slot, 2, r]
                )
            )
        return out

    for copy in copies(0, 0):
        copy.start()
    width = gate_buf.shape[-1]
    count = jnp.zeros((1, 128), jnp.float32)
    for tile in range(2 * SIDE):
        slot = tile % 2
        if tile + 1 < 2 * SIDE:
            for copy in copies(tile + 1, 1 - slot):
                copy.start()
        for copy in copies(tile, slot):
            copy.wait()
        lst, i = divmod(tile, SIDE)
        for y in range(SIDE):
            for x in range(SIDE):
                gate = gate_buf[slot, 0, y, x] + gate_buf[slot, 1, y, x] + gate_buf[slot, 2, y, x]
                up = up_buf[slot, 0, y, x] + up_buf[slot, 1, y, x] + up_buf[slot, 2, y, x]
                weight = route_buf[slot, y, x][:, :128]
                mask = route_buf[slot, y, x][:, 128:]
                count = count + jnp.sum(mask, axis=0, keepdims=True)
                weight = jnp.concatenate([weight] * (width // 128), axis=1)
                act = gate / (1.0 + jnp.exp(-gate)) * up * weight
                act = act.astype(jnp.bfloat16)
                ahead, behind = (i, y, x), (back(i), back(y), back(x))
                if lst == 0:
                    mine_ref[ahead + (0,)] = act
                    send_ref[behind + (1,)] = act
                else:
                    mine_ref[behind + (1,)] = act
                    send_ref[ahead + (0,)] = act
    count_ref[...] = count


def combine(gates, ups, route, tok, width):
    rows = jax.ShapeDtypeStruct((SIDE, SIDE, SIDE, 2, tok, width), jnp.bfloat16)
    return pl.pallas_call(
        combine_kernel,
        out_shape=(rows, rows, jax.ShapeDtypeStruct((1, 128), jnp.float32)),
        in_specs=[pl.BlockSpec(memory_space=pl.ANY)] * 56,
        out_specs=(
            pl.BlockSpec(memory_space=pltpu.VMEM),
            pl.BlockSpec(memory_space=pltpu.VMEM),
            pl.BlockSpec(memory_space=pltpu.VMEM),
        ),
        scratch_shapes=[
            pltpu.VMEM((2, 3, SIDE, SIDE, tok, width), jnp.float32),
            pltpu.VMEM((2, 3, SIDE, SIDE, tok, width), jnp.float32),
            pltpu.VMEM((2, SIDE, SIDE, tok, 256), jnp.float32),
            pltpu.SemaphoreType.DMA((2, 3, 9)),
        ],
        compiler_params=pltpu.CompilerParams(vmem_limit_bytes=32 * 1024 * 1024),
        name="combine",
    )(*gates, *ups, *route)


def cut(total, parts):
    tiles = total // 128
    sizes = [(tiles // parts + (1 if i < tiles % parts else 0)) * 128 for i in range(parts)]
    starts = [sum(sizes[:i]) for i in range(parts)]
    return list(zip(starts, sizes))


def on_device(tokens, routes, route_logits, gate_weight, up_weight, down_weight):
    tok, model = tokens.shape
    top_k = routes.shape[1]
    experts = lax.axis_size(EP)
    width = gate_weight.shape[2]
    half = model // 2
    core = lax.axis_index("c")
    expert = lax.axis_index(EP)
    gate_w, up_w, down_w = gate_weight[0], up_weight[0], down_weight[0]

    down_own = lax.dynamic_slice_in_dim(down_w, core * half, half, axis=1)
    down_peer = swap(lax.dynamic_slice_in_dim(down_w, (1 - core) * half, half, axis=1))

    whole = jnp.concatenate([tokens, route_columns(routes, route_logits, experts)], axis=1)
    thirds = cut(model + EXTRA, 3)
    current = [whole[:, s : s + n] for s, n in thirds]
    for stage in range(3):
        chains = [[c] for c in current]
        for _ in range(SIDE - 1):
            for t in range(3):
                chains[t].append(ring(chains[t][-1], GATHER[t][stage], 1))
        if stage < 2:
            current = [jnp.stack(c) for c in chains]
    peers = [[swap(b) for b in c] for c in chains]

    lanes = jnp.arange(EXTRA, dtype=jnp.int32)
    named = lanes % experts == expert
    pick = jnp.concatenate(
        [
            jnp.broadcast_to((named & (lanes >= experts))[:, None], (EXTRA, 128)),
            jnp.broadcast_to((named & (lanes < experts))[:, None], (EXTRA, 128)),
        ],
        axis=1,
    ).astype(jnp.bfloat16)

    def product(rows, weight):
        flat = rows.reshape(-1, rows.shape[-1])
        out = jnp.dot(flat, weight, preferred_element_type=jnp.float32)
        return out.reshape(*rows.shape[:-1], weight.shape[1])

    gates, ups, route = [], [], []
    for t, (s, n) in enumerate(thirds):
        real = min(n, model - s)
        for blocks in (chains[t], peers[t]):
            for b in blocks:
                gates.append(product(b[..., :real], gate_w[s : s + real]))
                ups.append(product(b[..., :real], up_w[s : s + real]))
                if real < n:
                    route.append(product(b[..., real:], pick))

    mine, to_peer, count = combine(gates, ups, route, tok, width)
    theirs = swap(to_peer)

    halves = []
    for (s, n), order in zip(cut(half, 3), REDUCE):
        own_w, peer_w = down_own[:, s : s + n], down_peer[:, s : s + n]

        def share(r, d=DIM[order[0]], own_w=own_w, peer_w=peer_w):
            return product(lax.index_in_dim(mine, r, d, False), own_w) + product(
                lax.index_in_dim(theirs, r, d, False), peer_w
            )

        left = list(order)
        names = ["z", "y", "x"]
        total = None
        for axis in order:
            d = names.index(axis)
            names.remove(axis)
            if total is None:
                piece = share
            else:
                piece = lambda r, total=total, d=d: lax.index_in_dim(total, r, d, False)
            moving = piece(SIDE - 1)
            for r in range(SIDE - 2, -1, -1):
                moving = ring(moving.astype(jnp.bfloat16), axis, -1).astype(jnp.float32) + piece(r)
            total = moving
        halves.append(total.astype(jnp.bfloat16))
    result = jnp.concatenate(halves, axis=-1)
    other = swap(result[1])
    mine_out = result[0]
    low = jnp.where(core == 0, mine_out, other)
    high = jnp.where(core == 0, other, mine_out)
    moe_output = jnp.concatenate([low, high], axis=1)
    mean_count = float(tok * lax.axis_size("x") * top_k)
    expert_load = count[0, :1] / mean_count
    return moe_output, expert_load


def solution(mesh):
    finer = Mesh(mesh.devices.reshape(SIDE, SIDE, 2, SIDE), EP_DP)
    in_specs = (
        P(EP_DP, None),
        P(EP_DP, None),
        P(EP_DP, None),
        P(EP, None, "x"),
        P(EP, None, "x"),
        P(EP, "x", None),
    )
    out_specs = (P(EP_DP, None), P(EP))
    return jax.shard_map(
        on_device, mesh=finer, in_specs=in_specs, out_specs=out_specs, check_vma=False
    )
```

```python
import jax
import jax.numpy as jnp
from jax import lax
from jax.experimental import pallas as pl
from jax.experimental.pallas import tpu as pltpu
from jax.sharding import Mesh
from jax.sharding import PartitionSpec as P

EP = ("z", "y", "c")
EP_DP = ("z", "y", "c", "x")
ROUTE_SCALE = 2.5
EXTRA = 128
SIDE = 4
GATHER = (("x", "y", "z"), ("y", "z", "x"), ("z", "x", "y"))
REDUCE = (("z", "y", "x"), ("x", "z", "y"), ("y", "x", "z"))


def pairwise(v, axis, turn):
    pairs = []
    for core in range(2):
        flip = 1 if core == turn else 3
        for i in range(SIDE):
            j = i ^ flip
            if axis == "x":
                pairs.append((core * SIDE + i, core * SIDE + j))
            else:
                pairs.append((i * 2 + core, j * 2 + core))
    return lax.ppermute(v, ("c", "x") if axis == "x" else (axis, "c"), pairs)


def swap(v):
    return lax.ppermute(v, "c", [(0, 1), (1, 0)])


def after(values, *others):
    return list(lax.optimization_barrier(tuple(values) + others)[: len(values)])


def route_columns(routes, route_logits, experts):
    affinity = jax.nn.sigmoid(route_logits)
    weights = ROUTE_SCALE * affinity / jnp.sum(affinity, axis=1, keepdims=True)
    hit = routes[:, :, None] == jnp.arange(experts, dtype=jnp.int32)[None, None, :]
    mask = jnp.sum(hit.astype(jnp.float32), axis=1)
    dense = jnp.sum(jnp.where(hit, weights[:, :, None], 0.0), axis=1)
    high = lax.reduce_precision(dense, 8, 7)
    rest = dense - high
    mid = lax.reduce_precision(rest, 8, 7)
    low = rest - mid
    return jnp.concatenate([mask, high, mid, low], axis=1).astype(jnp.bfloat16)


def combine_kernel(*refs):
    kinds = [refs[k * 12 : k * 12 + 12] for k in range(4)]
    route = refs[48:52]
    own_ref, peer_ref, count_ref = refs[52:55]
    buf, route_buf, sems = refs[55:]

    def copies(i, slot):
        out = []
        for k, parts in enumerate(kinds):
            first, second, third = parts[0:4], parts[4:8], parts[8:12]
            sem = sems.at[slot, k]
            out.append(pltpu.make_async_copy(first[i], buf.at[slot, k, 0], sem.at[0]))
            for r in range(SIDE):
                out.append(
                    pltpu.make_async_copy(second[r].at[i], buf.at[slot, k, 1, :, r], sem.at[1 + r])
                )
                out.append(
                    pltpu.make_async_copy(third[r].at[:, i], buf.at[slot, k, 2, r], sem.at[5 + r])
                )
        for r in range(SIDE):
            out.append(
                pltpu.make_async_copy(
                    route[r].at[:, i], route_buf.at[slot, r], sems.at[slot, 4, r]
                )
            )
        return out

    for copy in copies(0, 0):
        copy.start()
    width = buf.shape[-1]
    count_ref[...] = jnp.zeros_like(count_ref)
    for i in range(SIDE):
        slot = i % 2
        if i + 1 < SIDE:
            for copy in copies(i + 1, 1 - slot):
                copy.start()
        for copy in copies(i, slot):
            copy.wait()

        def block(n, carry, i=i, slot=slot):
            y, x = n // SIDE, n % SIDE
            sums = [buf[slot, k, 0, y, x] + buf[slot, k, 1, y, x] + buf[slot, k, 2, y, x] for k in range(4)]
            extra = route_buf[slot, y, x]
            for e, out in enumerate((own_ref, peer_ref)):
                gate, up = sums[2 * e], sums[2 * e + 1]
                weight = jnp.concatenate([extra[:, e * 128 : e * 128 + 128]] * (width // 128), axis=1)
                act = gate / (1.0 + jnp.exp(-gate)) * up * weight
                out[i, y, x] = act.astype(jnp.bfloat16)
            count_ref[...] += jnp.sum(extra[:, 256:], axis=0, keepdims=True)
            return carry

        lax.fori_loop(0, SIDE * SIDE, block, 0)


def combine(kinds, route, tok, width):
    rows = jax.ShapeDtypeStruct((SIDE, SIDE, SIDE, tok, width), jnp.bfloat16)
    return pl.pallas_call(
        combine_kernel,
        out_shape=(rows, rows, jax.ShapeDtypeStruct((1, 256), jnp.float32)),
        in_specs=[pl.BlockSpec(memory_space=pl.ANY)] * 52,
        out_specs=(pl.BlockSpec(memory_space=pltpu.VMEM),) * 3,
        scratch_shapes=[
            pltpu.VMEM((2, 4, 3, SIDE, SIDE, tok, width), jnp.float32),
            pltpu.VMEM((2, SIDE, SIDE, tok, 512), jnp.float32),
            pltpu.SemaphoreType.DMA((2, 5, 9)),
        ],
        compiler_params=pltpu.CompilerParams(vmem_limit_bytes=32 * 1024 * 1024),
        name="combine",
    )(*kinds[0], *kinds[1], *kinds[2], *kinds[3], *route)


def cut(total, parts):
    tiles = total // 128
    sizes = [(tiles // parts + (1 if i < tiles % parts else 0)) * 128 for i in range(parts)]
    starts = [sum(sizes[:i]) for i in range(parts)]
    return list(zip(starts, sizes))


def product(rows, weight):
    flat = rows.reshape(-1, rows.shape[-1])
    out = jnp.dot(flat, weight, preferred_element_type=jnp.float32)
    return out.reshape(*rows.shape[:-1], weight.shape[1])


def on_device(tokens, routes, route_logits, gate_weight, up_weight, down_weight):
    tok, model = tokens.shape
    top_k = routes.shape[1]
    experts = lax.axis_size(EP)
    width = gate_weight.shape[2]
    expert = lax.axis_index(EP)
    gate_w, up_w, down_w = gate_weight[0], up_weight[0], down_weight[0]

    gate_p = swap(gate_w)
    up_p = swap(after([up_w], gate_p)[0])
    down_p = swap(after([down_w], up_p)[0])

    whole = jnp.concatenate([tokens, route_columns(routes, route_logits, experts)], axis=1)
    thirds = cut(model + EXTRA, 3)
    current = [whole[:, s : s + n] for s, n in thirds]
    for stage in range(2):
        got = [pairwise(c, GATHER[t][stage], 0) for t, c in enumerate(current)]
        current = after([jnp.stack([c, g]) for c, g in zip(current, got)])
        got = [pairwise(c, GATHER[t][stage], 1) for t, c in enumerate(current)]
        current = after([jnp.concatenate([c, g]) for c, g in zip(current, got)])

    lanes = jnp.arange(EXTRA, dtype=jnp.int32)
    own, peer = lanes % experts == expert, lanes % experts == expert + 1 - 2 * lax.axis_index("c")
    columns = [own & (lanes >= experts), peer & (lanes >= experts)]
    columns += [own & (lanes < experts), peer & (lanes < experts)]
    pick = jnp.concatenate(
        [jnp.broadcast_to(c[:, None], (EXTRA, 128)) for c in columns], axis=1
    ).astype(jnp.bfloat16)

    def products(blocks):
        out, extra = [], None
        for (s, n), b in zip(thirds, blocks):
            real = min(n, model - s)
            out += [product(b[..., :real], w[s : s + real]) for w in (gate_w, up_w, gate_p, up_p)]
            if real < n:
                extra = product(b[..., real:], pick)
        return out + [extra]

    first = current
    results = []
    blocks = [first]
    got = [pairwise(c, GATHER[t][2], 0) for t, c in enumerate(first)]
    done = products(first)
    moved = after(got + first + done)
    got, first, done = moved[:3], moved[3:6], moved[6:]
    results.append(done)
    second = got
    got = [pairwise(c, GATHER[t][2], 1) for t, c in enumerate(first)]
    done = products(second)
    moved = after(got + second + done)
    got, second, done = moved[:3], moved[3:6], moved[6:]
    results.append(done)
    fetched = [pairwise(c, GATHER[t][2], 1) for t, c in enumerate(second)]
    done = products(got)
    moved = after(fetched + done)
    fetched, done = moved[:3], moved[3:]
    results.append(done)
    results.append(products(fetched))

    kinds = [[results[r][t * 4 + k] for t in range(3) for r in range(SIDE)] for k in range(4)]
    own_rows, peer_rows, count = combine(kinds, [results[r][12] for r in range(SIDE)], tok, width)

    sums = []
    for (s, n), order in zip(cut(model, 3), REDUCE):
        names = ["z", "y", "x"]
        total = None
        for axis in order:
            d = names.index(axis)
            names.remove(axis)
            if total is None:

                def piece(lo, d=d, s=s, n=n):
                    return product(
                        lax.slice_in_dim(own_rows, lo, lo + 2, axis=d), down_w[:, s : s + n]
                    ) + product(
                        lax.slice_in_dim(peer_rows, lo, lo + 2, axis=d), down_p[:, s : s + n]
                    )
            else:

                def piece(lo, d=d, total=total):
                    return lax.slice_in_dim(total, lo, lo + 2, axis=d)

            got = pairwise(piece(2).astype(jnp.bfloat16), axis, 1)
            total = piece(0) + got.astype(jnp.float32)
            got = pairwise(lax.index_in_dim(total, 1, d, False).astype(jnp.bfloat16), axis, 0)
            total = lax.index_in_dim(total, 0, d, False) + got.astype(jnp.float32)
        sums.append(total.astype(jnp.bfloat16))
    moe_output = jnp.concatenate(sums, axis=-1)
    counted = count[:, :128] + swap(count[:, 128:])
    mean_count = float(tok * lax.axis_size("x") * top_k)
    expert_load = counted[0, :1] / mean_count
    return moe_output, expert_load


def solution(mesh):
    finer = Mesh(mesh.devices.reshape(SIDE, SIDE, 2, SIDE), EP_DP)
    in_specs = (
        P(EP_DP, None),
        P(EP_DP, None),
        P(EP_DP, None),
        P(EP, None, "x"),
        P(EP, None, "x"),
        P(EP, "x", None),
    )
    out_specs = (P(EP_DP, None), P(EP))
    return jax.shard_map(
        on_device, mesh=finer, in_specs=in_specs, out_specs=out_specs, check_vma=False
    )
```

```python
import jax
import jax.numpy as jnp
from jax import lax
from jax.experimental import pallas as pl
from jax.experimental.pallas import tpu as pltpu
from jax.sharding import Mesh
from jax.sharding import PartitionSpec as P

EP = ("z", "y", "c")
EP_DP = ("z", "y", "c", "x")
ROUTE_SCALE = 2.5
EXTRA = 128
SIDE = 4
GATHER = (("x", "y", "z"), ("y", "z", "x"), ("z", "x", "y"))
REDUCE = (("z", "y", "x"), ("x", "z", "y"), ("y", "x", "z"))


def pairwise(v, axis, turn):
    pairs = []
    for core in range(2):
        flip = 1 if core == turn else 3
        for i in range(SIDE):
            j = i ^ flip
            if axis == "x":
                pairs.append((core * SIDE + i, core * SIDE + j))
            else:
                pairs.append((i * 2 + core, j * 2 + core))
    return lax.ppermute(v, ("c", "x") if axis == "x" else (axis, "c"), pairs)


def swap(v):
    return lax.ppermute(v, "c", [(0, 1), (1, 0)])


def after(values, *others):
    return list(lax.optimization_barrier(tuple(values) + others)[: len(values)])


def split(values):
    return values[:3], values[3:6], values[6]


def route_columns(routes, route_logits, experts):
    affinity = jax.nn.sigmoid(route_logits)
    weights = ROUTE_SCALE * affinity / jnp.sum(affinity, axis=1, keepdims=True)
    hit = routes[:, :, None] == jnp.arange(experts, dtype=jnp.int32)[None, None, :]
    mask = jnp.sum(hit.astype(jnp.float32), axis=1)
    dense = jnp.sum(jnp.where(hit, weights[:, :, None], 0.0), axis=1)
    high = lax.reduce_precision(dense, 8, 7)
    rest = dense - high
    mid = lax.reduce_precision(rest, 8, 7)
    low = rest - mid
    return jnp.concatenate([mask, high, mid, low], axis=1).astype(jnp.bfloat16)


def in_kernel(limits, t0, t1, t2, w0, w1, w2, w3, out, acc):
    j = pl.program_id(0)

    @pl.when((j == 0) | (j == limits[0]) | (j == limits[1]))
    def _():
        acc[...] = jnp.zeros_like(acc)

    flat = [t[...].reshape(acc.shape[1], t.shape[-1]) for t in (t0, t1, t2)]
    rows = jnp.where(j < limits[0], flat[0], jnp.where(j < limits[1], flat[1], flat[2]))
    for k, w in enumerate((w0, w1, w2, w3)):
        acc[k] += jnp.dot(rows, w[...], preferred_element_type=jnp.float32)

    @pl.when((j == limits[0] - 1) | (j == limits[1] - 1) | (j == limits[2] - 1))
    def _():
        out[0] = acc[...].astype(jnp.bfloat16).reshape(out.shape[1:])


def products(blocks, weights, starts, model, chunk):
    tok, width = blocks[0].shape[2], weights[0].shape[1]
    limits = (starts[1] // chunk, starts[2] // chunk, model // chunk)
    firsts = (0,) + limits[:2]
    tokens = [
        pl.BlockSpec(
            (SIDE, SIDE, tok, chunk),
            lambda j, lo=lo, hi=hi: (0, 0, 0, jnp.clip(j, lo, hi - 1) - lo),
        )
        for lo, hi in zip(firsts, limits)
    ]

    def third(j):
        return ((j >= limits[0]).astype(jnp.int32) + (j >= limits[1]).astype(jnp.int32), 0, 0, 0, 0, 0)

    return pl.pallas_call(
        lambda *refs: in_kernel(limits, *refs),
        out_shape=jax.ShapeDtypeStruct((3, 4, SIDE, SIDE, tok, width), jnp.bfloat16),
        grid=(model // chunk,),
        in_specs=tokens + [pl.BlockSpec((chunk, width), lambda j: (j, 0))] * 4,
        out_specs=pl.BlockSpec((1, 4, SIDE, SIDE, tok, width), third),
        scratch_shapes=[pltpu.VMEM((4, SIDE * SIDE * tok, width), jnp.float32)],
        name="products",
    )(*blocks, *weights)


def combine_kernel(start, *refs):
    parts, extras = refs[:4], refs[4:8]
    pick_ref = refs[8]
    own_ref, peer_ref, count_ref = refs[9:12]
    buf, extra_buf, route_buf, sems = refs[12:]

    def copies(i, slot):
        sem = sems.at[slot]
        out = [pltpu.make_async_copy(parts[i].at[0], buf.at[slot, :, 0], sem.at[0])]
        for r in range(SIDE):
            out.append(
                pltpu.make_async_copy(parts[r].at[1, :, i], buf.at[slot, :, 1, :, r], sem.at[1 + r])
            )
            out.append(
                pltpu.make_async_copy(parts[r].at[2, :, :, i], buf.at[slot, :, 2, r], sem.at[5 + r])
            )
            out.append(
                pltpu.make_async_copy(
                    extras[r].at[:, i, :, start : start + EXTRA], extra_buf.at[slot, r], sem.at[9 + r]
                )
            )
        return out

    for copy in copies(0, 0):
        copy.start()
    tok, width = buf.shape[-2:]
    count_ref[...] = jnp.zeros_like(count_ref)
    for i in range(SIDE):
        slot = i % 2
        if i + 1 < SIDE:
            for copy in copies(i + 1, 1 - slot):
                copy.start()
        for copy in copies(i, slot):
            copy.wait()
        extra = extra_buf[slot].reshape(SIDE * SIDE * tok, EXTRA)
        route = jnp.dot(extra, pick_ref[...], preferred_element_type=jnp.float32)
        count_ref[...] += jnp.sum(route[:, 256:], axis=0, keepdims=True)
        route_buf[...] = route[:, :256].reshape(route_buf.shape)

        def block(n, carry, i=i, slot=slot):
            y, x = n // SIDE, n % SIDE
            sums = []
            for k in range(4):
                three = [buf[slot, k, t, y, x].astype(jnp.float32) for t in range(3)]
                sums.append(three[0] + three[1] + three[2])
            weights = route_buf[y, x]
            for e, out in enumerate((own_ref, peer_ref)):
                gate, up = sums[2 * e], sums[2 * e + 1]
                weight = weights[:, e * 128 : e * 128 + 128]
                weight = jnp.concatenate([weight] * (width // 128), axis=1)
                act = gate / (1.0 + jnp.exp(-gate)) * up * weight
                out[i, y, x] = act.astype(jnp.bfloat16)
            return carry

        lax.fori_loop(0, SIDE * SIDE, block, 0)


def combine(parts, extras, pick, start):
    tok, width = parts[0].shape[-2:]
    rows = jax.ShapeDtypeStruct((SIDE, SIDE, SIDE, tok, width), jnp.bfloat16)
    return pl.pallas_call(
        lambda *refs: combine_kernel(start, *refs),
        out_shape=(rows, rows, jax.ShapeDtypeStruct((1, 256), jnp.float32)),
        in_specs=[pl.BlockSpec(memory_space=pl.ANY)] * 8 + [pl.BlockSpec(memory_space=pltpu.VMEM)],
        out_specs=(pl.BlockSpec(memory_space=pltpu.VMEM),) * 3,
        scratch_shapes=[
            pltpu.VMEM((2, 4, 3, SIDE, SIDE, tok, width), jnp.bfloat16),
            pltpu.VMEM((2, SIDE, SIDE, tok, EXTRA), jnp.bfloat16),
            pltpu.VMEM((SIDE, SIDE, tok, 256), jnp.float32),
            pltpu.SemaphoreType.DMA((2, 13)),
        ],
        name="combine",
    )(*parts, *extras, pick)


def down_kernel(d, lo, added, own_ref, peer_ref, own_w, peer_w, *refs):
    for p in range(2):
        index = (slice(None),) * d + (lo + p,)
        flat = own_ref[index].reshape(-1, own_ref.shape[-1])
        total = jnp.dot(flat, own_w[...], preferred_element_type=jnp.float32)
        flat = peer_ref[index].reshape(-1, peer_ref.shape[-1])
        total = total + jnp.dot(flat, peer_w[...], preferred_element_type=jnp.float32)
        if added:
            got, outs = refs[0], refs[1:]
            total = total + got[p].astype(jnp.float32)
            outs[p][...] = total.astype(outs[p].dtype)
        else:
            refs[0][p] = total.astype(jnp.bfloat16)


def down(own_rows, peer_rows, own_w, peer_w, d, lo, start, size, chunk, got=None):
    tok, width = own_rows.shape[-2:]
    count = SIDE * SIDE * tok
    whole = pl.BlockSpec(own_rows.shape, lambda j: (0,) * 5)
    weight = pl.BlockSpec((width, chunk), lambda j: (0, start // chunk + j))
    pair = pl.BlockSpec((2, count, chunk), lambda j: (0, 0, j))
    one = pl.BlockSpec((count, chunk), lambda j: (0, j))
    operands, specs = [own_rows, peer_rows, own_w, peer_w], [whole, whole, weight, weight]
    if got is None:
        out_shape, out_specs = jax.ShapeDtypeStruct((2, count, size), jnp.bfloat16), pair
    else:
        operands, specs = operands + [got], specs + [pair]
        out_shape = (
            jax.ShapeDtypeStruct((count, size), jnp.float32),
            jax.ShapeDtypeStruct((count, size), jnp.bfloat16),
        )
        out_specs = (one, one)
    return pl.pallas_call(
        lambda *refs: down_kernel(d, lo, got is not None, *refs),
        out_shape=out_shape,
        grid=(size // chunk,),
        in_specs=specs,
        out_specs=out_specs,
        compiler_params=pltpu.CompilerParams(vmem_limit_bytes=32 * 1024 * 1024),
        name="down",
    )(*operands)


def cut(total, chunk):
    tiles = total // chunk
    sizes = [(tiles // 3 + (1 if i < tiles % 3 else 0)) * chunk for i in range(3)]
    return [sum(sizes[:i]) for i in range(3)], sizes


def on_device(tokens, routes, route_logits, gate_weight, up_weight, down_weight):
    tok, model = tokens.shape
    top_k = routes.shape[1]
    experts = lax.axis_size(EP)
    width = gate_weight.shape[2]
    expert = lax.axis_index(EP)
    gate_w, up_w, down_w = gate_weight[0], up_weight[0], down_weight[0]

    gate_p = swap(gate_w)
    up_p = swap(after([up_w], gate_p)[0])
    down_p = swap(after([down_w], up_p)[0])

    chunk = min(512, model // 3 // 128 * 128)
    starts, sizes = cut(model, chunk)
    whole = jnp.concatenate([tokens, route_columns(routes, route_logits, experts)], axis=1)
    stops = starts[1:] + [model + EXTRA]
    current = [whole[:, lo:hi] for lo, hi in zip(starts, stops)]
    for stage in range(2):
        got = [pairwise(c, GATHER[t][stage], 0) for t, c in enumerate(current)]
        current = after([jnp.stack([c, g]) for c, g in zip(current, got)])
        got = [pairwise(c, GATHER[t][stage], 1) for t, c in enumerate(current)]
        current = after([jnp.concatenate([c, g]) for c, g in zip(current, got)])

    lanes = jnp.arange(EXTRA, dtype=jnp.int32)
    own, peer = lanes % experts == expert, lanes % experts == expert + 1 - 2 * lax.axis_index("c")
    columns = [own & (lanes >= experts), peer & (lanes >= experts)]
    columns += [own & (lanes < experts), peer & (lanes < experts)]
    pick = jnp.concatenate(
        [jnp.broadcast_to(c[:, None], (EXTRA, 128)) for c in columns], axis=1
    ).astype(jnp.bfloat16)

    def part(blocks):
        return products(blocks, (gate_w, up_w, gate_p, up_p), starts, model, chunk)

    def moved(blocks, turn):
        return [pairwise(b, GATHER[t][2], turn) for t, b in enumerate(blocks)]

    me = current
    first, p0 = moved(me, 0), part(me)
    first, me, p0 = split(after(first + me + [p0]))
    second, p1 = moved(me, 1), part(first)
    second, first, p1 = split(after(second + first + [p1]))
    both, p2 = moved(first, 1), part(second)
    both, second, p2 = split(after(both + second + [p2]))
    parts = [p0, p1, p2, part(both)]
    extras = [me[2], first[2], second[2], both[2]]
    own_rows, peer_rows, count = combine(parts, extras, pick, model - starts[2])

    weights = (own_rows, peer_rows, down_w, down_p)
    names = [["z", "y", "x"] for _ in REDUCE]

    def traded(values, level, turn):
        got = [pairwise(v, order[level], turn) for v, order in zip(values, REDUCE)]
        return [after([g], *values)[0] for g in got]

    sides = [n.index(order[0]) for n, order in zip(names, REDUCE)]
    spans = list(zip(sides, starts, sizes))
    sent = [down(*weights, d, 2, start, size, chunk) for d, start, size in spans]
    got = traded(sent, 0, 1)
    both = [down(*weights, d, 0, start, size, chunk, g) for (d, start, size), g in zip(spans, got)]
    got = traded([last for _, last in both], 0, 0)
    totals = []
    for (total, _), g, n, order, size in zip(both, got, names, REDUCE, sizes):
        n.remove(order[0])
        totals.append((total + g.astype(jnp.float32)).reshape(SIDE, SIDE, tok, size))
    for level in (1, 2):
        sides = [n.index(order[level]) for n, order in zip(names, REDUCE)]
        sent = [lax.slice_in_dim(v, 2, 4, axis=d).astype(jnp.bfloat16) for v, d in zip(totals, sides)]
        got = traded(sent, level, 1)
        totals = [
            lax.slice_in_dim(v, 0, 2, axis=d) + g.astype(jnp.float32)
            for v, g, d in zip(totals, got, sides)
        ]
        sent = [lax.index_in_dim(v, 1, d, False).astype(jnp.bfloat16) for v, d in zip(totals, sides)]
        got = traded(sent, level, 0)
        totals = [
            lax.index_in_dim(v, 0, d, False) + g.astype(jnp.float32)
            for v, g, d in zip(totals, got, sides)
        ]
        for n, order in zip(names, REDUCE):
            n.remove(order[level])
    moe_output = jnp.concatenate([v.astype(jnp.bfloat16) for v in totals], axis=-1)
    counted = count[:, :128] + swap(count[:, 128:])
    mean_count = float(tok * lax.axis_size("x") * top_k)
    expert_load = counted[0, :1] / mean_count
    return moe_output, expert_load


def solution(mesh):
    finer = Mesh(mesh.devices.reshape(SIDE, SIDE, 2, SIDE), EP_DP)
    in_specs = (
        P(EP_DP, None),
        P(EP_DP, None),
        P(EP_DP, None),
        P(EP, None, "x"),
        P(EP, None, "x"),
        P(EP, "x", None),
    )
    out_specs = (P(EP_DP, None), P(EP))
    return jax.shard_map(
        on_device, mesh=finer, in_specs=in_specs, out_specs=out_specs, check_vma=False
    )
```

```python
import jax
import jax.numpy as jnp
from jax import lax
from jax.experimental import pallas as pl
from jax.experimental.pallas import tpu as pltpu
from jax.sharding import Mesh
from jax.sharding import PartitionSpec as P

EP = ("z", "y", "c")
EP_DP = ("z", "y", "c", "x")
ROUTE_SCALE = 2.5
EXTRA = 128
SIDE = 4
GATHER = (("x", "y", "z"), ("y", "z", "x"), ("z", "x", "y"))
REDUCE = (("z", "y", "x"), ("x", "z", "y"), ("y", "x", "z"))


def pairwise(v, axis, turn):
    pairs = []
    for core in range(2):
        flip = 1 if core == turn else 3
        for i in range(SIDE):
            j = i ^ flip
            if axis == "x":
                pairs.append((core * SIDE + i, core * SIDE + j))
            else:
                pairs.append((i * 2 + core, j * 2 + core))
    return lax.ppermute(v, ("c", "x") if axis == "x" else (axis, "c"), pairs)


def swap(v):
    return lax.ppermute(v, "c", [(0, 1), (1, 0)])


def after(values, *others):
    return list(lax.optimization_barrier(tuple(values) + others)[: len(values)])


def split(values):
    return values[:3], values[3:6], values[6]


def route_columns(routes, route_logits, experts):
    affinity = jax.nn.sigmoid(route_logits)
    weights = ROUTE_SCALE * affinity / jnp.sum(affinity, axis=1, keepdims=True)
    hit = routes[:, :, None] == jnp.arange(experts, dtype=jnp.int32)[None, None, :]
    mask = jnp.sum(hit.astype(jnp.float32), axis=1)
    mask = mask + swap(mask)
    dense = jnp.sum(jnp.where(hit, weights[:, :, None], 0.0), axis=1)
    high = lax.reduce_precision(dense, 8, 7)
    rest = dense - high
    mid = lax.reduce_precision(rest, 8, 7)
    low = rest - mid
    return jnp.concatenate([mask, high, mid, low], axis=1).astype(jnp.bfloat16)


def products_kernel(starts, sizes, *refs):
    blocks, weights, out = refs[:3], refs[3:7], refs[7]
    rows_buf, weight_buf, out_buf, rows_sem, weight_sem, out_sem = refs[8:]
    size, rest = sizes[0], sizes[2]

    def rows_copy(t):
        return pltpu.make_async_copy(
            blocks[t].at[:, :, :, : sizes[t]], rows_buf.at[t, :, :, :, : sizes[t]], rows_sem.at[t]
        )

    def full(t, k):
        source = weights[k].at[pl.ds(pl.multiple_of(t * size, 128), size)]
        return pltpu.make_async_copy(source, weight_buf.at[k, :size], weight_sem.at[k])

    def tail(k):
        source = weights[k].at[starts[2] : starts[2] + rest]
        return pltpu.make_async_copy(source, weight_buf.at[k, :rest], weight_sem.at[k])

    def out_copy(t, k):
        return pltpu.make_async_copy(out_buf.at[k % 2], out.at[t, k], out_sem.at[k % 2])

    def store(t, k, cols, wait):
        rows = rows_buf[t, :, :, :, :cols].reshape(-1, cols)
        total = jnp.dot(rows, weight_buf[k, :cols], preferred_element_type=jnp.float32)
        wait()
        out_buf[k % 2] = total.astype(jnp.bfloat16).reshape(out_buf.shape[1:])
        out_copy(t, k).start()

    rows_copy(0).start()
    for k in range(3):
        full(0, k).start()
    rows_copy(1).start()
    rows_copy(2).start()
    rows_copy(0).wait()

    def third(t, carry):
        for k in range(4):
            full(t, k).wait()
            if k == 0:
                full(t, 3).start()
            else:
                pl.when(t == 0)(full(1, k - 1).start)
                pl.when(t == 1)(tail(k - 1).start)
            last = out_copy(t, k).wait
            store(t, k, size, last if k >= 2 else lambda last=last: pl.when(t > 0)(last))
        pl.when(t == 0)(rows_copy(1).wait)
        return carry

    lax.fori_loop(0, 2, third, 0)
    rows_copy(2).wait()
    for k in range(4):
        tail(k).wait()
        if k == 0:
            tail(3).start()
        store(2, k, rest, out_copy(2, k).wait)
    out_copy(2, 2).wait()
    out_copy(2, 3).wait()


def products(blocks, weights, starts, sizes):
    tok, width = blocks[0].shape[2], weights[0].shape[1]
    longest = max(sizes)
    return pl.pallas_call(
        lambda *refs: products_kernel(starts, sizes, *refs),
        out_shape=jax.ShapeDtypeStruct((3, 4, SIDE, SIDE, tok, width), jnp.bfloat16),
        in_specs=[pl.BlockSpec(memory_space=pl.ANY)] * 7,
        out_specs=pl.BlockSpec(memory_space=pl.ANY),
        scratch_shapes=[
            pltpu.VMEM((3, SIDE, SIDE, tok, longest), jnp.bfloat16),
            pltpu.VMEM((4, longest, width), jnp.bfloat16),
            pltpu.VMEM((2, SIDE, SIDE, tok, width), jnp.bfloat16),
            pltpu.SemaphoreType.DMA((3,)),
            pltpu.SemaphoreType.DMA((4,)),
            pltpu.SemaphoreType.DMA((2,)),
        ],
        name="products",
    )(*blocks, *weights)


def combine_kernel(start, *refs):
    parts, extras = refs[:4], refs[4:8]
    pick_ref = refs[8]
    own_ref, peer_ref, count_ref = refs[9:12]
    buf, extra_buf, route_buf, sems = refs[12:]

    def copies(i, slot):
        sem = sems.at[slot]
        out = [pltpu.make_async_copy(parts[i].at[0], buf.at[slot, :, 0], sem.at[0])]
        for r in range(SIDE):
            out.append(
                pltpu.make_async_copy(parts[r].at[1, :, i], buf.at[slot, :, 1, :, r], sem.at[1 + r])
            )
            out.append(
                pltpu.make_async_copy(parts[r].at[2, :, :, i], buf.at[slot, :, 2, r], sem.at[5 + r])
            )
            out.append(
                pltpu.make_async_copy(
                    extras[r].at[:, i, :, start : start + EXTRA], extra_buf.at[slot, r], sem.at[9 + r]
                )
            )
        return out

    for copy in copies(0, 0):
        copy.start()
    tok, width = buf.shape[-2:]
    count_ref[...] = jnp.zeros_like(count_ref)
    for i in range(SIDE):
        slot = i % 2
        if i + 1 < SIDE:
            for copy in copies(i + 1, 1 - slot):
                copy.start()
        for copy in copies(i, slot):
            copy.wait()
        extra = extra_buf[slot].reshape(SIDE * SIDE * tok, EXTRA)
        route = jnp.dot(extra, pick_ref[...], preferred_element_type=jnp.float32)
        count_ref[...] += jnp.sum(route[:, 256:], axis=0, keepdims=True)
        route_buf[...] = route[:, :256].reshape(route_buf.shape)

        def block(n, carry, i=i, slot=slot):
            y, x = n // SIDE, n % SIDE
            sums = []
            for k in range(4):
                three = [buf[slot, k, t, y, x].astype(jnp.float32) for t in range(3)]
                sums.append(three[0] + three[1] + three[2])
            weights = route_buf[y, x]
            for e, out in enumerate((own_ref, peer_ref)):
                gate, up = sums[2 * e], sums[2 * e + 1]
                weight = weights[:, e * 128 : e * 128 + 128]
                weight = jnp.concatenate([weight] * (width // 128), axis=1)
                act = gate / (1.0 + jnp.exp(-gate)) * up * weight
                out[i, y, x] = act.astype(jnp.bfloat16)
            return carry

        lax.fori_loop(0, SIDE * SIDE, block, 0)


def combine(parts, extras, pick, start):
    tok, width = parts[0].shape[-2:]
    rows = jax.ShapeDtypeStruct((SIDE, SIDE, SIDE, tok, width), jnp.bfloat16)
    return pl.pallas_call(
        lambda *refs: combine_kernel(start, *refs),
        out_shape=(rows, rows, jax.ShapeDtypeStruct((1, 128), jnp.float32)),
        in_specs=[pl.BlockSpec(memory_space=pl.ANY)] * 8 + [pl.BlockSpec(memory_space=pltpu.VMEM)],
        out_specs=(pl.BlockSpec(memory_space=pltpu.VMEM),) * 3,
        scratch_shapes=[
            pltpu.VMEM((2, 4, 3, SIDE, SIDE, tok, width), jnp.bfloat16),
            pltpu.VMEM((2, SIDE, SIDE, tok, EXTRA), jnp.bfloat16),
            pltpu.VMEM((SIDE, SIDE, tok, 256), jnp.float32),
            pltpu.SemaphoreType.DMA((2, 13)),
        ],
        name="combine",
    )(*parts, *extras, pick)


def down_kernel(d, lo, added, own_ref, peer_ref, own_w, peer_w, *refs):
    index = (slice(None),) * d + (slice(lo, lo + 2),)
    own = own_ref[index]
    shape = own.shape[:-1] + own_w.shape[1:]
    total = jnp.dot(
        own.reshape(-1, own.shape[-1]), own_w[...], preferred_element_type=jnp.float32
    ) + jnp.dot(
        peer_ref[index].reshape(-1, own.shape[-1]), peer_w[...], preferred_element_type=jnp.float32
    )
    if added:
        got, outs = refs[0], refs[1:]
        total = (total + got[...].astype(jnp.float32)).reshape(shape)
        for p, out in enumerate(outs):
            part = total[(slice(None),) * d + (p,)]
            out[...] = part.reshape(out.shape).astype(out.dtype)
    else:
        refs[0][...] = total.astype(jnp.bfloat16)


def down(own_rows, peer_rows, own_w, peer_w, d, lo, start, size, chunk, got=None):
    tok, width = own_rows.shape[-2:]
    count = SIDE * SIDE * tok
    whole = pl.BlockSpec(own_rows.shape, lambda j: (0,) * 5)
    weight = pl.BlockSpec((width, chunk), lambda j: (0, start // chunk + j))
    pair = pl.BlockSpec((2 * count, chunk), lambda j: (0, j))
    one = pl.BlockSpec((count, chunk), lambda j: (0, j))
    operands, specs = [own_rows, peer_rows, own_w, peer_w], [whole, whole, weight, weight]
    limit = None if got is None else 24 * 1024 * 1024
    if got is None:
        out_shape, out_specs = jax.ShapeDtypeStruct((2 * count, size), jnp.bfloat16), pair
    else:
        operands, specs = operands + [got], specs + [pair]
        out_shape = (
            jax.ShapeDtypeStruct((count, size), jnp.float32),
            jax.ShapeDtypeStruct((count, size), jnp.bfloat16),
        )
        out_specs = (one, one)
    return pl.pallas_call(
        lambda *refs: down_kernel(d, lo, got is not None, *refs),
        out_shape=out_shape,
        grid=(size // chunk,),
        in_specs=specs,
        out_specs=out_specs,
        compiler_params=pltpu.CompilerParams(vmem_limit_bytes=limit),
        name="down",
    )(*operands)


def cut(total, chunk):
    tiles = total // chunk
    sizes = [(tiles // 3 + (1 if i < tiles % 3 else 0)) * chunk for i in range(3)]
    return [sum(sizes[:i]) for i in range(3)], sizes


def on_device(tokens, routes, route_logits, gate_weight, up_weight, down_weight):
    tok, model = tokens.shape
    top_k = routes.shape[1]
    experts = lax.axis_size(EP)
    width = gate_weight.shape[2]
    expert = lax.axis_index(EP)
    gate_w, up_w, down_w = gate_weight[0], up_weight[0], down_weight[0]

    chunk = min(512, model // 3 // 128 * 128)
    starts, sizes = cut(model, chunk)
    whole = jnp.concatenate([tokens, route_columns(routes, route_logits, experts)], axis=1)
    stops = starts[1:] + [model + EXTRA]
    current = [whole[:, lo:hi] for lo, hi in zip(starts, stops)]
    swapped = []
    for stage, weight in enumerate((gate_w, up_w)):
        weight, *current = after([weight] + current)
        other = swap(weight)
        got = [pairwise(c, GATHER[t][stage], 0) for t, c in enumerate(current)]
        current = after([jnp.stack([c, g]) for c, g in zip(current, got)])
        got = [pairwise(c, GATHER[t][stage], 1) for t, c in enumerate(current)]
        *current, other = after([jnp.concatenate([c, g]) for c, g in zip(current, got)] + [other])
        swapped.append(other)
    gate_p, up_p = swapped

    lanes = jnp.arange(EXTRA, dtype=jnp.int32)
    own, peer = lanes % experts == expert, lanes % experts == expert + 1 - 2 * lax.axis_index("c")
    columns = [own & (lanes >= experts), peer & (lanes >= experts), own & (lanes < experts)]
    pick = jnp.concatenate(
        [jnp.broadcast_to(c[:, None], (EXTRA, 128)) for c in columns], axis=1
    ).astype(jnp.bfloat16)

    def part(blocks):
        return products(blocks, (gate_w, up_w, gate_p, up_p), starts, sizes)

    def moved(blocks, turn):
        return [pairwise(b, GATHER[t][2], turn) for t, b in enumerate(blocks)]

    me = current
    down_p = swap(after([down_w], *me)[0])
    first, p0 = moved(me, 0), part(me)
    first, me, p0 = split(after(first + me + [p0]))
    second, p1 = moved(me, 1), part(first)
    second, first, p1 = split(after(second + first + [p1]))
    both, p2 = moved(first, 1), part(second)
    both, second, p2 = split(after(both + second + [p2]))
    parts = [p0, p1, p2, part(both)]
    extras = [me[2], first[2], second[2], both[2]]
    own_rows, peer_rows, count = combine(parts, extras, pick, model - starts[2])

    weights = (own_rows, peer_rows, down_w, down_p)
    names = [["z", "y", "x"] for _ in REDUCE]

    def traded(values, level, turn):
        got = [pairwise(v, order[level], turn) for v, order in zip(values, REDUCE)]
        return [after([g], *values)[0] for g in got]

    sides = [n.index(order[0]) for n, order in zip(names, REDUCE)]
    spans = list(zip(sides, starts, sizes))
    sent = [down(*weights, d, 2, start, size, size // 2) for d, start, size in spans]
    got = traded(sent, 0, 1)
    both = [down(*weights, d, 0, start, size, chunk, g) for (d, start, size), g in zip(spans, got)]
    got = traded([last for _, last in both], 0, 0)
    totals = []
    for (total, _), g, n, order, size in zip(both, got, names, REDUCE, sizes):
        n.remove(order[0])
        totals.append((total + g.astype(jnp.float32)).reshape(SIDE, SIDE, tok, size))
    for level in (1, 2):
        sides = [n.index(order[level]) for n, order in zip(names, REDUCE)]
        sent = [lax.slice_in_dim(v, 2, 4, axis=d).astype(jnp.bfloat16) for v, d in zip(totals, sides)]
        got = traded(sent, level, 1)
        totals = [
            lax.slice_in_dim(v, 0, 2, axis=d) + g.astype(jnp.float32)
            for v, g, d in zip(totals, got, sides)
        ]
        sent = [lax.index_in_dim(v, 1, d, False).astype(jnp.bfloat16) for v, d in zip(totals, sides)]
        got = traded(sent, level, 0)
        totals = [
            lax.index_in_dim(v, 0, d, False) + g.astype(jnp.float32)
            for v, g, d in zip(totals, got, sides)
        ]
        for n, order in zip(names, REDUCE):
            n.remove(order[level])
    moe_output = jnp.concatenate([v.astype(jnp.bfloat16) for v in totals], axis=-1)
    mean_count = float(tok * lax.axis_size("x") * top_k)
    expert_load = count[0, :1] / mean_count
    return moe_output, expert_load


def solution(mesh):
    finer = Mesh(mesh.devices.reshape(SIDE, SIDE, 2, SIDE), EP_DP)
    in_specs = (
        P(EP_DP, None),
        P(EP_DP, None),
        P(EP_DP, None),
        P(EP, None, "x"),
        P(EP, None, "x"),
        P(EP, "x", None),
    )
    out_specs = (P(EP_DP, None), P(EP))
    return jax.shard_map(
        on_device, mesh=finer, in_specs=in_specs, out_specs=out_specs, check_vma=False
    )
```

```python
import jax
import jax.numpy as jnp
from jax import lax
from jax.experimental import pallas as pl
from jax.experimental.pallas import tpu as pltpu
from jax.sharding import Mesh
from jax.sharding import PartitionSpec as P

EP = ("z", "y", "c")
EP_DP = ("z", "y", "c", "x")
ROUTE_SCALE = 2.5
EXTRA = 128
SIDE = 4
GATHER = (("x", "y", "z"), ("y", "z", "x"), ("z", "x", "y"))
REDUCE = (("z", "y", "x"), ("x", "z", "y"), ("y", "x", "z"))


def pairwise(v, axis, turn):
    pairs = []
    for core in range(2):
        flip = 1 if core == turn else 3
        for i in range(SIDE):
            j = i ^ flip
            if axis == "x":
                pairs.append((core * SIDE + i, core * SIDE + j))
            else:
                pairs.append((i * 2 + core, j * 2 + core))
    return lax.ppermute(v, ("c", "x") if axis == "x" else (axis, "c"), pairs)


def swap(v):
    return lax.ppermute(v, "c", [(0, 1), (1, 0)])


def after(values, *others):
    return list(lax.optimization_barrier(tuple(values) + others)[: len(values)])


def route_columns(routes, route_logits, experts):
    affinity = jax.nn.sigmoid(route_logits)
    weights = ROUTE_SCALE * affinity / jnp.sum(affinity, axis=1, keepdims=True)
    hit = routes[:, :, None] == jnp.arange(experts, dtype=jnp.int32)[None, None, :]
    mask = jnp.sum(hit.astype(jnp.float32), axis=1)
    mask = mask + swap(mask)
    dense = jnp.sum(jnp.where(hit, weights[:, :, None], 0.0), axis=1)
    high = lax.reduce_precision(dense, 8, 7)
    rest = dense - high
    mid = lax.reduce_precision(rest, 8, 7)
    low = rest - mid
    return jnp.concatenate([mask, high, mid, low], axis=1).astype(jnp.bfloat16)


def products_kernel(starts, sizes, *refs):
    blocks, weights, out = refs[:3], refs[3:7], refs[7]
    rows_buf, weight_buf, out_buf, rows_sem, weight_sem, out_sem = refs[8:]
    size, rest = sizes[0], sizes[2]

    def rows_copy(t):
        return pltpu.make_async_copy(
            blocks[t].at[:, :, :, :, : sizes[t]],
            rows_buf.at[t, :, :, :, :, : sizes[t]],
            rows_sem.at[t],
        )

    def full(t, k):
        source = weights[k].at[pl.ds(pl.multiple_of(t * size, 128), size)]
        return pltpu.make_async_copy(source, weight_buf.at[k, :size], weight_sem.at[k])

    def tail(k):
        source = weights[k].at[starts[2] : starts[2] + rest]
        return pltpu.make_async_copy(source, weight_buf.at[k, :rest], weight_sem.at[k])

    def out_copy(t, k):
        return pltpu.make_async_copy(out_buf.at[k % 2], out.at[t, k], out_sem.at[k % 2])

    def store(t, k, cols, wait):
        rows = rows_buf[t, :, :, :, :, :cols].reshape(-1, cols)
        total = jnp.dot(rows, weight_buf[k, :cols], preferred_element_type=jnp.float32)
        wait()
        out_buf[k % 2] = total.astype(jnp.bfloat16).reshape(out_buf.shape[1:])
        out_copy(t, k).start()

    rows_copy(0).start()
    for k in range(3):
        full(0, k).start()
    rows_copy(1).start()
    rows_copy(2).start()
    rows_copy(0).wait()

    def third(t, carry):
        for k in range(4):
            full(t, k).wait()
            if k == 0:
                full(t, 3).start()
            else:
                pl.when(t == 0)(full(1, k - 1).start)
                pl.when(t == 1)(tail(k - 1).start)
            last = out_copy(t, k).wait
            store(t, k, size, last if k >= 2 else lambda last=last: pl.when(t > 0)(last))
        pl.when(t == 0)(rows_copy(1).wait)
        return carry

    lax.fori_loop(0, 2, third, 0)
    rows_copy(2).wait()
    for k in range(4):
        tail(k).wait()
        if k == 0:
            tail(3).start()
        store(2, k, rest, out_copy(2, k).wait)
    out_copy(2, 2).wait()
    out_copy(2, 3).wait()


def products(blocks, weights, starts, sizes):
    tok, width = blocks[0].shape[3], weights[0].shape[1]
    longest = max(sizes)
    return pl.pallas_call(
        lambda *refs: products_kernel(starts, sizes, *refs),
        out_shape=jax.ShapeDtypeStruct((3, 4, 2, SIDE, SIDE, tok, width), jnp.bfloat16),
        in_specs=[pl.BlockSpec(memory_space=pl.ANY)] * 7,
        out_specs=pl.BlockSpec(memory_space=pl.ANY),
        scratch_shapes=[
            pltpu.VMEM((3, 2, SIDE, SIDE, tok, longest), jnp.bfloat16),
            pltpu.VMEM((4, longest, width), jnp.bfloat16),
            pltpu.VMEM((2, 2, SIDE, SIDE, tok, width), jnp.bfloat16),
            pltpu.SemaphoreType.DMA((3,)),
            pltpu.SemaphoreType.DMA((4,)),
            pltpu.SemaphoreType.DMA((2,)),
        ],
        name="products",
    )(*blocks, *weights)


def down_steps(plan, lo, own_rows, peer_rows, own_w, peer_w, outs, bufs):
    dims, sizes, chunk = plan
    weight_buf, out_buf, weight_sem, out_sem = bufs
    blocks = [size // chunk for size in sizes]
    total = sum(blocks)

    def fetch(c):
        slot = c % 3
        columns = pl.ds(pl.multiple_of(c * chunk, chunk), chunk)
        return [
            pltpu.make_async_copy(w.at[:, columns], weight_buf.at[slot, e], weight_sem.at[slot, e])
            for e, w in enumerate((own_w, peer_w))
        ]

    def begin():
        for c in range(2):
            for copy in fetch(c):
                copy.start()

    def finish():
        first = 0
        for d, count, out in zip(dims, blocks, outs):
            index = (slice(None),) * d + (slice(lo, lo + 2),)

            def save(c, j, out=out):
                columns = pl.ds(pl.multiple_of(j * chunk, chunk), chunk)
                return pltpu.make_async_copy(
                    out_buf.at[c % 2], out.at[:, columns], out_sem.at[c % 2]
                )

            def step(j, carry, first=first, index=index, save=save):
                c = first + j
                for copy in fetch(c):
                    copy.wait()

                @pl.when(c + 2 < total)
                def _():
                    for copy in fetch(c + 2):
                        copy.start()

                value = None
                for e, rows in enumerate((own_rows, peer_rows)):
                    flat = rows[index]
                    flat = flat.reshape(-1, flat.shape[-1])
                    term = jnp.dot(flat, weight_buf[c % 3, e], preferred_element_type=jnp.float32)
                    value = term if value is None else value + term
                pl.when(c >= 2)(save(c, j).wait)
                out_buf[c % 2] = value.astype(jnp.bfloat16)
                save(c, j).start()
                return carry

            lax.fori_loop(0, count, step, 0)
            first += count
        save(total - 2, blocks[-1] - 2).wait()
        save(total - 1, blocks[-1] - 1).wait()

    return begin, finish


def down_scratch(count, width, chunk):
    return [
        pltpu.VMEM((3, 2, width, chunk), jnp.bfloat16),
        pltpu.VMEM((2, count, chunk), jnp.bfloat16),
        pltpu.SemaphoreType.DMA((3, 2)),
        pltpu.SemaphoreType.DMA((2,)),
    ]


def combine_kernel(start, plan, *refs):
    parts, extras, pick_ref = refs[:2], refs[2:4], refs[4]
    own_w, peer_w = refs[5:7]
    own_out, peer_out, count_ref, *sends = refs[7:13]
    buf, extra_buf, route_buf, own_ref, peer_ref, sems, rows_sem = refs[13:20]
    begin, finish = down_steps(plan, 2, own_ref, peer_ref, own_w, peer_w, sends, refs[20:])

    def copies(i, slot):
        sem = sems.at[slot]
        out = [pltpu.make_async_copy(parts[i // 2].at[0, :, i % 2], buf.at[slot, :, 0], sem.at[0])]
        for r in range(SIDE):
            out.append(
                pltpu.make_async_copy(
                    parts[r // 2].at[1, :, r % 2, i], buf.at[slot, :, 1, :, r], sem.at[1 + r]
                )
            )
            out.append(
                pltpu.make_async_copy(
                    parts[r // 2].at[2, :, r % 2, :, i], buf.at[slot, :, 2, r], sem.at[5 + r]
                )
            )
            out.append(
                pltpu.make_async_copy(
                    extras[r // 2].at[r % 2, :, i, :, start : start + EXTRA],
                    extra_buf.at[slot, r],
                    sem.at[9 + r],
                )
            )
        return out

    for copy in copies(0, 0):
        copy.start()
    tok, width = buf.shape[-2:]
    count_ref[...] = jnp.zeros_like(count_ref)
    for i in range(SIDE):
        slot = i % 2
        if i + 1 < SIDE:
            for copy in copies(i + 1, 1 - slot):
                copy.start()
        else:
            begin()
        for copy in copies(i, slot):
            copy.wait()
        extra = extra_buf[slot].reshape(SIDE * SIDE * tok, EXTRA)
        route = jnp.dot(extra, pick_ref[...], preferred_element_type=jnp.float32)
        count_ref[...] += jnp.sum(route[:, 256:], axis=0, keepdims=True)
        route_buf[...] = route[:, :256].reshape(route_buf.shape)

        def block(n, carry, i=i, slot=slot):
            y, x = n // SIDE, n % SIDE
            sums = []
            for k in range(4):
                three = [buf[slot, k, t, y, x].astype(jnp.float32) for t in range(3)]
                sums.append(three[0] + three[1] + three[2])
            weights = route_buf[y, x]
            for e, out in enumerate((own_ref, peer_ref)):
                gate, up = sums[2 * e], sums[2 * e + 1]
                weight = weights[:, e * 128 : e * 128 + 128]
                weight = jnp.concatenate([weight] * (width // 128), axis=1)
                act = gate / (1.0 + jnp.exp(-gate)) * up * weight
                out[i, y, x] = act.astype(jnp.bfloat16)
            return carry

        lax.fori_loop(0, SIDE * SIDE, block, 0)
    kept = [
        pltpu.make_async_copy(own_ref, own_out, rows_sem.at[0]),
        pltpu.make_async_copy(peer_ref, peer_out, rows_sem.at[1]),
    ]
    for copy in kept:
        copy.start()
    finish()
    for copy in kept:
        copy.wait()


def combine(parts, extras, pick, start, own_w, peer_w, plan):
    tok, width = parts[0].shape[-2:]
    rows = jax.ShapeDtypeStruct((SIDE, SIDE, SIDE, tok, width), jnp.bfloat16)
    count = 2 * SIDE * SIDE * tok
    anywhere = pl.BlockSpec(memory_space=pl.ANY)
    inside = pl.BlockSpec(memory_space=pltpu.VMEM)
    return pl.pallas_call(
        lambda *refs: combine_kernel(start, plan, *refs),
        out_shape=(rows, rows, jax.ShapeDtypeStruct((1, 128), jnp.float32))
        + tuple(jax.ShapeDtypeStruct((count, size), jnp.bfloat16) for size in plan[1]),
        in_specs=[anywhere] * 4 + [inside] + [anywhere] * 2,
        out_specs=(anywhere, anywhere, inside) + (anywhere,) * 3,
        scratch_shapes=[
            pltpu.VMEM((2, 4, 3, SIDE, SIDE, tok, width), jnp.bfloat16),
            pltpu.VMEM((2, SIDE, SIDE, tok, EXTRA), jnp.bfloat16),
            pltpu.VMEM((SIDE, SIDE, tok, 256), jnp.float32),
            pltpu.VMEM(rows.shape, jnp.bfloat16),
            pltpu.VMEM(rows.shape, jnp.bfloat16),
            pltpu.SemaphoreType.DMA((2, 13)),
            pltpu.SemaphoreType.DMA((2,)),
        ]
        + down_scratch(count, width, plan[2]),
        name="combine",
    )(*parts, *extras, pick, own_w, peer_w)


def keep_kernel(plan, own_ref, peer_ref, own_w, peer_w, *refs):
    begin, finish = down_steps(plan, 0, own_ref, peer_ref, own_w, peer_w, refs[:3], refs[3:])
    begin()
    finish()


def keep(own_rows, peer_rows, own_w, peer_w, plan):
    tok, width = own_rows.shape[-2:]
    count = 2 * SIDE * SIDE * tok
    anywhere = pl.BlockSpec(memory_space=pl.ANY)
    inside = pl.BlockSpec(memory_space=pltpu.VMEM)
    return pl.pallas_call(
        lambda *refs: keep_kernel(plan, *refs),
        out_shape=tuple(jax.ShapeDtypeStruct((count, size), jnp.bfloat16) for size in plan[1]),
        in_specs=[inside] * 2 + [anywhere] * 2,
        out_specs=(anywhere,) * 3,
        scratch_shapes=down_scratch(count, width, plan[2]),
        name="keep",
    )(own_rows, peer_rows, own_w, peer_w)


def cut(total, chunk):
    tiles = total // chunk
    sizes = [(tiles // 3 + (1 if i < tiles % 3 else 0)) * chunk for i in range(3)]
    return [sum(sizes[:i]) for i in range(3)], sizes


def on_device(tokens, routes, route_logits, gate_weight, up_weight, down_weight):
    tok, model = tokens.shape
    top_k = routes.shape[1]
    experts = lax.axis_size(EP)
    width = gate_weight.shape[2]
    expert = lax.axis_index(EP)
    gate_w, up_w, down_w = gate_weight[0], up_weight[0], down_weight[0]

    chunk = min(512, model // 3 // 128 * 128)
    starts, sizes = cut(model, chunk)
    whole = jnp.concatenate([tokens, route_columns(routes, route_logits, experts)], axis=1)
    stops = starts[1:] + [model + EXTRA]
    current = [whole[:, lo:hi] for lo, hi in zip(starts, stops)]
    swapped = []
    for stage, weight in enumerate((gate_w, up_w)):
        weight, *current = after([weight] + current)
        other = swap(weight)
        got = [pairwise(c, GATHER[t][stage], 0) for t, c in enumerate(current)]
        current = after([jnp.stack([c, g]) for c, g in zip(current, got)])
        got = [pairwise(c, GATHER[t][stage], 1) for t, c in enumerate(current)]
        *current, other = after([jnp.concatenate([c, g]) for c, g in zip(current, got)] + [other])
        swapped.append(other)
    gate_p, up_p = swapped

    lanes = jnp.arange(EXTRA, dtype=jnp.int32)
    own, peer = lanes % experts == expert, lanes % experts == expert + 1 - 2 * lax.axis_index("c")
    columns = [own & (lanes >= experts), peer & (lanes >= experts), own & (lanes < experts)]
    pick = jnp.concatenate(
        [jnp.broadcast_to(c[:, None], (EXTRA, 128)) for c in columns], axis=1
    ).astype(jnp.bfloat16)

    def part(blocks):
        return products(blocks, (gate_w, up_w, gate_p, up_p), starts, sizes)

    def moved(blocks, turn):
        return [pairwise(b, GATHER[t][2], turn) for t, b in enumerate(blocks)]

    me = current
    down_p = swap(after([down_w], *me)[0])
    near = moved(me, 0)
    near = after([jnp.stack([m, f]) for m, f in zip(me, near)])
    far, p0 = moved(near, 1), part(near)
    *far, p0 = after(far + [p0])
    p1 = part(far)

    names = ["z", "y", "x"]
    dims = tuple(names.index(order[0]) for order in REDUCE)
    plan = (dims, tuple(sizes), chunk)
    own_rows, peer_rows, count, *sent = combine(
        (p0, p1), (near[2], far[2]), pick, model - starts[2], down_w, down_p, plan
    )

    def traded(values, level, turn):
        got = [pairwise(v, order[level], turn) for v, order in zip(values, REDUCE)]
        return [after([g], *values)[0] for g in got]

    def summed(terms):
        total = terms[0].astype(jnp.float32)
        for term in terms[1:]:
            total = total + term.astype(jnp.float32)
        return total.astype(jnp.bfloat16)

    got = traded(sent, 0, 1)
    kept = keep(own_rows, peer_rows, down_w, down_p, plan)
    terms, left = [], []
    for k, g, d, size, order in zip(kept, got, dims, sizes, REDUCE):
        shape = [SIDE] * d + [2] + [SIDE] * (2 - d) + [tok, size]
        terms.append([k.reshape(shape), g.reshape(shape)])
        left.append(list(names))
    for level in range(3):
        sides = [n.index(order[level]) for n, order in zip(left, REDUCE)]
        if level:
            sent = [
                summed([lax.slice_in_dim(v, 2, 4, axis=d) for v in vs]) for vs, d in zip(terms, sides)
            ]
            got = traded(sent, level, 1)
            terms = [
                [lax.slice_in_dim(v, 0, 2, axis=d) for v in vs] + [g]
                for vs, g, d in zip(terms, got, sides)
            ]
        sent = [
            summed([lax.index_in_dim(v, 1, d, False) for v in vs]) for vs, d in zip(terms, sides)
        ]
        got = traded(sent, level, 0)
        terms = [
            [lax.index_in_dim(v, 0, d, False) for v in vs] + [g]
            for vs, g, d in zip(terms, got, sides)
        ]
        for n, order in zip(left, REDUCE):
            n.remove(order[level])
    moe_output = jnp.concatenate([summed(vs) for vs in terms], axis=-1)
    mean_count = float(tok * lax.axis_size("x") * top_k)
    expert_load = count[0, :1] / mean_count
    return moe_output, expert_load


def solution(mesh):
    finer = Mesh(mesh.devices.reshape(SIDE, SIDE, 2, SIDE), EP_DP)
    in_specs = (
        P(EP_DP, None),
        P(EP_DP, None),
        P(EP_DP, None),
        P(EP, None, "x"),
        P(EP, None, "x"),
        P(EP, "x", None),
    )
    out_specs = (P(EP_DP, None), P(EP))
    return jax.shard_map(
        on_device, mesh=finer, in_specs=in_specs, out_specs=out_specs, check_vma=False
    )
```
